32 devices in a mesh: group: 2 (over x), xline: 16 (over z, y, core).
Axes of the slice: x: 2, y: 2, z: 4, core: 2. Of those that a mesh axis runs over, the one named last changes fastest.
Arguments:
- tokens: bfloat16 [128, 256, 1024], P('group', 'xline'), parts along dimension 0, may hold values from -6 to 6
- norm_gain: float32 [1024], replicated, may hold values from 0.1 to 1.9
- norm_bias: float32 [1024], replicated, may hold values from -3 to 3
- w_qkv: bfloat16 [1024, 3072], replicated, may hold values from -0.1875 to 0.1875
- w_out: bfloat16 [1024, 1024], replicated, may hold values from -0.1875 to 0.1875
Outputs:
- mixed: bfloat16 [128, 256, 1024], P('group', 'xline'), parts along dimension 0
The draws below stay inside these ranges and needn't reach their ends.
There are 2 independent parts, one for each index of `group`. The reference program is written for one: setup_inputs(seed, part) draws one part's arguments, and reference() takes and returns one part's arrays. A program takes and returns all parts, laid end to end along the dimension named above; an argument that names none is the same for every part. Nothing has to cross between parts.
All inputs are finite; a program needn't handle non-finite values.
Results may differ from the reference program's by a relative error of at most 0.005.
Values may be sent and summed in bfloat16 or wider, within the bound.
A program may use at most 192 MiB of HBM per device.

```python
import jax
import jax.numpy as jnp
from jax import lax

D = 1024
H = 16
HD = 64
INL = 64
XL = 256


def levels(key, dims, split, low, high):
    level, own = 1.0, jax.random.fold_in(key, 6)
    for position, blocks in split:
        heights = jnp.exp(jax.random.uniform(jax.random.fold_in(own, position), (blocks,), jnp.float32, low / len(split), high / len(split)))
        level = level * jnp.repeat(heights, dims[position] // blocks).reshape([-1 if axis == position else 1 for axis in range(len(dims))])
    return level


def centred(key, shape, scale, bound, pieces=(), kind=jnp.bfloat16):
    values = jax.random.normal(key, shape, jnp.float32) * scale
    if len(pieces) > 0:
        values = levels(key, shape, pieces, -0.22, 0.18) * values
    return jnp.clip(values, min=-bound, max=bound).astype(kind)


def setup_inputs(seed: int = 0, part: int = 0) -> dict:
    key_list = jax.random.split(jax.random.key(seed), 6)
    part_keys = jax.random.split(jax.random.fold_in(key_list[5], part), 6)
    return {
        "tokens": centred(part_keys[0], (INL, XL, D), 1.0, 6.0, ((1, 16),)),
        "norm_gain": jnp.clip(1.0 + 0.18 * jax.random.normal(key_list[1], (D,), jnp.float32), 0.1, 1.9),
        "norm_bias": centred(key_list[2], (D,), 0.5, 3.0, (), jnp.float32),
        "w_qkv": centred(key_list[3], (D, 3 * D), D ** -0.5, 0.1875),
        "w_out": centred(key_list[4], (D, D), D ** -0.5, 0.1875),
    }


def layer_norm(tokens, norm_gain, norm_bias):
    values = tokens.astype(jnp.float32)
    center = lax.optimization_barrier(jnp.mean(values, axis=-1, keepdims=True))
    spread = lax.optimization_barrier(jnp.mean((values - center) ** 2, axis=-1, keepdims=True))
    return ((values - center) * lax.rsqrt(spread + 1e-05) * norm_gain + norm_bias).astype(jnp.bfloat16)

def attend_row(row_qkv):
    width = row_qkv.shape[-1] // 3
    length = row_qkv.shape[0]
    query = row_qkv[:, :width].reshape(length, H, HD).astype(jnp.float32)
    keys = row_qkv[:, width:2 * width].reshape(length, H, HD).astype(jnp.float32)
    values = row_qkv[:, 2 * width:].reshape(length, H, HD).astype(jnp.float32)
    scores = jnp.einsum('chd,thd->hct', query, keys) / jnp.sqrt(jnp.float32(HD))
    probs = jax.nn.softmax(scores, axis=-1).astype(jnp.bfloat16)
    result = jnp.einsum('hct,thd->chd', probs.astype(jnp.float32), values)
    return result.astype(jnp.bfloat16).reshape(length, width)

def reference(tokens, norm_gain, norm_bias, w_qkv, w_out):
    normed = layer_norm(tokens, norm_gain, norm_bias)
    flat = normed.reshape(-1, D)
    qkv = jnp.dot(flat, w_qkv, preferred_element_type=jnp.float32).astype(jnp.bfloat16)
    qkv = qkv.reshape(INL, XL, 3 * D)
    attended = lax.map(attend_row, qkv)
    projected = jnp.dot(attended.reshape(-1, D), w_out, preferred_element_type=jnp.float32).astype(jnp.bfloat16)
    mixed = tokens.astype(jnp.float32) + projected.reshape(INL, XL, D).astype(jnp.float32)
    return mixed.astype(jnp.bfloat16)
```

```python
import functools

import jax
import jax.numpy as jnp
from jax import lax
from jax.experimental import pallas as pl
from jax.experimental.pallas import tpu as pltpu
from jax.sharding import PartitionSpec as P

HD = 64
PAIR = 2 * HD
BLOCK = 256
WIDE = 512
LANES = 4
F32 = jnp.float32
BF16 = jnp.bfloat16


def remote(src, dst, send_sem, recv_sem, peer):
    return pltpu.make_async_remote_copy(
        src_ref=src,
        dst_ref=dst,
        send_sem=send_sem,
        recv_sem=recv_sem,
        device_id={"xline": peer},
        device_id_type=pl.DeviceIdType.MESH,
    )


def kernel(
    n, rows, cols, width,
    tok, gain_hbm, bias_hbm, w_qkv_hbm, w_out_hbm, out,
    recv, res, gain, bias, w_qkv, w_out, normed, qkv, att,
    in_send, in_recv, out_send, out_recv, w_sem, ready,
):
    me = lax.axis_index("xline")
    length = n * cols
    block = min(BLOCK, length)
    per = block // cols

    loads = [
        pltpu.make_async_copy(far, near, w_sem.at[i])
        for i, (far, near) in enumerate(
            ((w_qkv_hbm, w_qkv), (w_out_hbm, w_out), (gain_hbm, gain), (bias_hbm, bias))
        )
    ]

    def all_of(ref, sem):
        return pltpu.make_async_copy(ref, ref, sem)

    def each_peer(body, unroll=False):
        half = n // 2
        side = me // half

        @pl.loop(0, half, unroll=unroll)
        def _(k):
            depth = half - 1 - k
            peer = jnp.where(side == 0, half + depth, half - 1 - depth)
            body(peer - lax.rem(peer, 4) + lax.rem(me + peer, 4))

        @pl.loop(1, half, unroll=unroll)
        def _(k):
            body(side * half + lax.rem(me + k, half))

    barrier = pltpu.get_barrier_semaphore()
    half = n // 2
    inner = jnp.logical_and(me >= half - LANES, me < half + LANES)
    across = jnp.where(me < half, me + LANES, me - LANES)
    partners = (across, across + 1 - 2 * lax.rem(across, 2))

    def greet(peer, sem=barrier):
        pl.semaphore_signal(
            sem, inc=1, device_id={"xline": peer}, device_id_type=pl.DeviceIdType.MESH
        )

    def send_row(r, peer):
        remote(
            tok.at[peer * rows + r], recv.at[r, me], in_send.at[0], in_recv.at[r], peer
        ).start()

    @pl.when(inner)
    def _():
        for peer in partners:
            greet(peer)

    @pl.loop(0, n - 2 * LANES)
    def _(k):
        peer = jnp.where(k < half - LANES, k, k + 2 * LANES)

        @pl.when(peer != me)
        def _():
            greet(peer)

    @pl.when(inner)
    def _():
        pl.semaphore_wait(barrier, 2)
        for r in range(rows):
            for peer in partners:
                send_row(r, peer)

    @pl.loop(0, rows)
    def _(r):
        pltpu.make_async_copy(tok.at[me * rows + r], recv.at[r, me], in_recv.at[r]).start()

    @pl.when(jnp.logical_not(inner))
    def _():
        pl.semaphore_wait(barrier, n - 1)
        side = jnp.where(me < half, 1, -1)
        near = me + side * LANES

        @pl.when(jnp.logical_and(near >= half - LANES, near < half + LANES))
        def _():
            greet(near, ready)

    @pl.when(inner)
    def _():
        pl.semaphore_wait(ready, 1)

    @pl.loop(0, rows)
    def _(r):
        def send(peer):
            done = jnp.logical_and(inner, peer // 2 == across // 2)

            @pl.when(jnp.logical_not(done))
            def _():
                send_row(r, peer)

        each_peer(send, unroll=True)

    for load in loads:
        load.start()
    for load in loads:
        load.wait()
    low = lax.broadcasted_iota(jnp.int32, (1, PAIR), 1) < HD

    @pl.loop(0, rows)
    def _(r):
        all_of(recv.at[r], in_recv.at[r]).wait()

        @pl.loop(0, length // block)
        def _(b):
            here = pl.ds(pl.multiple_of(b * block, block), block)
            values = recv[r, pl.ds(b * per, per)].astype(F32).reshape(block, width)
            center = jnp.mean(values, axis=-1, keepdims=True)
            moved = values - center
            spread = jnp.mean(moved * moved, axis=-1, keepdims=True)
            normed[...] = (moved * lax.rsqrt(spread + 1e-05) * gain[...] + bias[...]).astype(BF16)

            @pl.loop(0, 3 * width // WIDE)
            def _(c):
                at = pl.ds(pl.multiple_of(c * WIDE, WIDE), WIDE)
                qkv[here, at] = jnp.dot(
                    normed[...], w_qkv[:, at], preferred_element_type=F32
                ).astype(BF16)

        @pl.loop(0, length // block)
        def _(b):
            here = pl.ds(pl.multiple_of(b * block, block), block)

            @pl.loop(0, width // PAIR)
            def _(h):
                q = qkv[here, pl.ds(pl.multiple_of(h * PAIR, PAIR), PAIR)].astype(F32) * 0.125
                keys = qkv[:, pl.ds(pl.multiple_of(width + h * PAIR, PAIR), PAIR)]
                vals = qkv[:, pl.ds(pl.multiple_of(2 * width + h * PAIR, PAIR), PAIR)]
                halves = []
                for mask in (low, jnp.logical_not(low)):
                    one = jnp.where(mask, q, 0.0).astype(BF16)
                    scores = lax.dot_general(
                        one, keys, (((1,), (1,)), ((), ())), preferred_element_type=F32
                    )
                    top = jnp.max(scores, axis=-1, keepdims=True)
                    weights = jnp.exp(scores - top)
                    total = jnp.sum(weights, axis=-1, keepdims=True)
                    mixed = jnp.dot(weights.astype(BF16), vals, preferred_element_type=F32)
                    halves.append(mixed / total)
                att[:, pl.ds(pl.multiple_of(h * PAIR, PAIR), PAIR)] = jnp.where(
                    low, halves[0], halves[1]
                ).astype(BF16)

            @pl.loop(0, width // WIDE)
            def _(c):
                at = pl.ds(pl.multiple_of(c * WIDE, WIDE), WIDE)
                projected = jnp.dot(
                    att[...], w_out[:, at], preferred_element_type=F32
                ).astype(BF16)
                tokens = recv[r, pl.ds(b * per, per), :, at].astype(F32)
                res[r, pl.ds(b * per, per), :, at] = (
                    tokens + projected.astype(F32).reshape(per, cols, WIDE)
                ).astype(BF16)

        pltpu.make_async_copy(res.at[r, me], out.at[me * rows + r], out_recv.at[0]).start()

        def send(peer):
            remote(
                res.at[r, peer], out.at[me * rows + r], out_send.at[0], out_recv.at[0], peer
            ).start()

        each_peer(send)

    sent = tok.at[pl.ds(0, rows * (n - 1))]
    all_of(sent, in_send.at[0]).wait()
    all_of(sent, out_send.at[0]).wait()
    all_of(out, out_recv.at[0]).wait()


def on_device(tokens, norm_gain, norm_bias, w_qkv, w_out):
    inline_rows, cols, width = tokens.shape
    n = lax.axis_size("xline")
    rows = inline_rows // n
    length = n * cols
    anywhere = pl.BlockSpec(memory_space=pl.ANY)
    dma = pltpu.SemaphoreType.DMA
    return pl.pallas_call(
        functools.partial(kernel, n, rows, cols, width),
        out_shape=pltpu.VMEM(tokens.shape, tokens.dtype),
        in_specs=[pl.BlockSpec(memory_space=pltpu.HBM)] * 5,
        out_specs=pl.BlockSpec(memory_space=pltpu.VMEM),
        scratch_shapes=[
            pltpu.VMEM((rows, n, cols, width), BF16),
            pltpu.VMEM((rows, n, cols, width), BF16),
            pltpu.VMEM((1, width), F32),
            pltpu.VMEM((1, width), F32),
            pltpu.VMEM(w_qkv.shape, BF16),
            pltpu.VMEM(w_out.shape, BF16),
            pltpu.VMEM((min(BLOCK, length), width), BF16),
            pltpu.VMEM((length, 3 * width), BF16),
            pltpu.VMEM((min(BLOCK, length), width), BF16),
            dma((1,)),
            dma((rows,)),
            dma((1,)),
            dma((1,)),
            dma((4,)),
            pltpu.SemaphoreType.REGULAR,
        ],
        compiler_params=pltpu.CompilerParams(
            collective_id=0, has_side_effects=True, vmem_limit_bytes=52 * 2**20
        ),
    )(tokens, norm_gain.reshape(1, width), norm_bias.reshape(1, width), w_qkv, w_out)


def solution(mesh):
    in_specs = (P("group", "xline", None), P(), P(), P(), P())
    out_specs = P("group", "xline", None)
    return jax.shard_map(
        on_device, mesh=mesh, in_specs=in_specs, out_specs=out_specs, check_vma=False
    )
```

```python
import functools

import jax
import jax.numpy as jnp
from jax import lax
from jax.experimental import pallas as pl
from jax.experimental.pallas import tpu as pltpu
from jax.sharding import PartitionSpec as P

HD = 64
PAIR = 2 * HD
BLOCK = 256
WIDE = 512
LANES = 4
F32 = jnp.float32
BF16 = jnp.bfloat16


def remote(src, dst, send_sem, recv_sem, peer):
    return pltpu.make_async_remote_copy(
        src_ref=src,
        dst_ref=dst,
        send_sem=send_sem,
        recv_sem=recv_sem,
        device_id={"xline": peer},
        device_id_type=pl.DeviceIdType.MESH,
    )


def kernel(
    n, rows, cols, width,
    tok, gain_hbm, bias_hbm, w_qkv_hbm, w_out_hbm, out,
    recv, res, gain, bias, w_qkv, w_out, normed, qkv, att,
    in_send, in_recv, out_send, out_recv, w_sem, ready,
):
    me = lax.axis_index("xline")
    length = n * cols
    block = min(BLOCK, length)
    per = block // cols

    loads = [
        pltpu.make_async_copy(far, near, w_sem.at[i])
        for i, (far, near) in enumerate(
            ((w_qkv_hbm, w_qkv), (w_out_hbm, w_out), (gain_hbm, gain), (bias_hbm, bias))
        )
    ]

    def all_of(ref, sem):
        return pltpu.make_async_copy(ref, ref, sem)

    def each_peer(body, unroll=False):
        half = n // 2
        side = me // half

        @pl.loop(0, half, unroll=unroll)
        def _(k):
            depth = half - 1 - k
            peer = jnp.where(side == 0, half + depth, half - 1 - depth)
            lane = lax.rem(me, 4)
            q = lax.rem(k, 4)
            lane = 2 * lax.rem(lane // 2 + 1 - q // 2, 2) + lax.rem(lane + q, 2)
            body(peer - lax.rem(peer, 4) + lane)

        @pl.loop(1, half, unroll=unroll)
        def _(k):
            body(side * half + lax.rem(me + k, half))

    barrier = pltpu.get_barrier_semaphore()
    half = n // 2
    inner = jnp.logical_and(me >= half - LANES, me < half + LANES)
    across = jnp.where(me < half, me + LANES, me - LANES)
    partners = (across, across + 1 - 2 * lax.rem(across, 2))

    def greet(peer, sem=barrier):
        pl.semaphore_signal(
            sem, inc=1, device_id={"xline": peer}, device_id_type=pl.DeviceIdType.MESH
        )

    def send_row(r, peer):
        remote(
            tok.at[peer * rows + r], recv.at[r, me], in_send.at[0], in_recv.at[r], peer
        ).start()

    @pl.when(inner)
    def _():
        for peer in partners:
            greet(peer)

    @pl.loop(0, n - 2 * LANES)
    def _(k):
        peer = jnp.where(k < half - LANES, k, k + 2 * LANES)

        @pl.when(peer != me)
        def _():
            greet(peer)

    @pl.when(inner)
    def _():
        pl.semaphore_wait(barrier, 2)
        for r in range(rows):
            for peer in partners:
                send_row(r, peer)

    @pl.loop(0, rows)
    def _(r):
        pltpu.make_async_copy(tok.at[me * rows + r], recv.at[r, me], in_recv.at[r]).start()

    @pl.when(jnp.logical_not(inner))
    def _():
        pl.semaphore_wait(barrier, n - 1)
        side = jnp.where(me < half, 1, -1)
        near = me + side * LANES

        @pl.when(jnp.logical_and(near >= half - LANES, near < half + LANES))
        def _():
            greet(near, ready)

    @pl.when(inner)
    def _():
        pl.semaphore_wait(ready, 1)

    @pl.loop(0, rows)
    def _(r):
        def send(peer):
            done = jnp.logical_and(inner, peer // 2 == across // 2)

            @pl.when(jnp.logical_not(done))
            def _():
                send_row(r, peer)

        each_peer(send, unroll=True)

    for load in loads:
        load.start()
    for load in loads:
        load.wait()
    low = lax.broadcasted_iota(jnp.int32, (1, PAIR), 1) < HD

    @pl.loop(0, rows)
    def _(r):
        all_of(recv.at[r], in_recv.at[r]).wait()

        @pl.loop(0, length // block)
        def _(b):
            here = pl.ds(pl.multiple_of(b * block, block), block)
            values = recv[r, pl.ds(b * per, per)].astype(F32).reshape(block, width)
            center = jnp.mean(values, axis=-1, keepdims=True)
            moved = values - center
            spread = jnp.mean(moved * moved, axis=-1, keepdims=True)
            normed[...] = (moved * lax.rsqrt(spread + 1e-05) * gain[...] + bias[...]).astype(BF16)

            @pl.loop(0, 3 * width // WIDE)
            def _(c):
                at = pl.ds(pl.multiple_of(c * WIDE, WIDE), WIDE)
                qkv[here, at] = jnp.dot(
                    normed[...], w_qkv[:, at], preferred_element_type=F32
                ).astype(BF16)

        @pl.loop(0, length // block)
        def _(b):
            here = pl.ds(pl.multiple_of(b * block, block), block)

            @pl.loop(0, width // PAIR)
            def _(h):
                q = qkv[here, pl.ds(pl.multiple_of(h * PAIR, PAIR), PAIR)].astype(F32) * 0.125
                keys = qkv[:, pl.ds(pl.multiple_of(width + h * PAIR, PAIR), PAIR)]
                vals = qkv[:, pl.ds(pl.multiple_of(2 * width + h * PAIR, PAIR), PAIR)]
                halves = []
                for mask in (low, jnp.logical_not(low)):
                    one = jnp.where(mask, q, 0.0).astype(BF16)
                    scores = lax.dot_general(
                        one, keys, (((1,), (1,)), ((), ())), preferred_element_type=F32
                    )
                    top = jnp.max(scores, axis=-1, keepdims=True)
                    weights = jnp.exp(scores - top)
                    total = jnp.sum(weights, axis=-1, keepdims=True)
                    mixed = jnp.dot(weights.astype(BF16), vals, preferred_element_type=F32)
                    halves.append(mixed / total)
                att[:, pl.ds(pl.multiple_of(h * PAIR, PAIR), PAIR)] = jnp.where(
                    low, halves[0], halves[1]
                ).astype(BF16)

            @pl.loop(0, width // WIDE)
            def _(c):
                at = pl.ds(pl.multiple_of(c * WIDE, WIDE), WIDE)
                projected = jnp.dot(
                    att[...], w_out[:, at], preferred_element_type=F32
                ).astype(BF16)
                tokens = recv[r, pl.ds(b * per, per), :, at].astype(F32)
                res[r, pl.ds(b * per, per), :, at] = (
                    tokens + projected.astype(F32).reshape(per, cols, WIDE)
                ).astype(BF16)

        pltpu.make_async_copy(res.at[r, me], out.at[me * rows + r], out_recv.at[0]).start()

        def send(peer):
            remote(
                res.at[r, peer], out.at[me * rows + r], out_send.at[0], out_recv.at[0], peer
            ).start()

        each_peer(send)

    sent = tok.at[pl.ds(0, rows * (n - 1))]
    all_of(sent, in_send.at[0]).wait()
    all_of(sent, out_send.at[0]).wait()
    all_of(out, out_recv.at[0]).wait()


def on_device(tokens, norm_gain, norm_bias, w_qkv, w_out):
    inline_rows, cols, width = tokens.shape
    n = lax.axis_size("xline")
    rows = inline_rows // n
    length = n * cols
    anywhere = pl.BlockSpec(memory_space=pl.ANY)
    dma = pltpu.SemaphoreType.DMA
    return pl.pallas_call(
        functools.partial(kernel, n, rows, cols, width),
        out_shape=pltpu.VMEM(tokens.shape, tokens.dtype),
        in_specs=[pl.BlockSpec(memory_space=pltpu.HBM)] * 5,
        out_specs=pl.BlockSpec(memory_space=pltpu.VMEM),
        scratch_shapes=[
            pltpu.VMEM((rows, n, cols, width), BF16),
            pltpu.VMEM((rows, n, cols, width), BF16),
            pltpu.VMEM((1, width), F32),
            pltpu.VMEM((1, width), F32),
            pltpu.VMEM(w_qkv.shape, BF16),
            pltpu.VMEM(w_out.shape, BF16),
            pltpu.VMEM((min(BLOCK, length), width), BF16),
            pltpu.VMEM((length, 3 * width), BF16),
            pltpu.VMEM((min(BLOCK, length), width), BF16),
            dma((1,)),
            dma((rows,)),
            dma((1,)),
            dma((1,)),
            dma((4,)),
            pltpu.SemaphoreType.REGULAR,
        ],
        compiler_params=pltpu.CompilerParams(
            collective_id=0, has_side_effects=True, vmem_limit_bytes=52 * 2**20
        ),
    )(tokens, norm_gain.reshape(1, width), norm_bias.reshape(1, width), w_qkv, w_out)


def solution(mesh):
    in_specs = (P("group", "xline", None), P(), P(), P(), P())
    out_specs = P("group", "xline", None)
    return jax.shard_map(
        on_device, mesh=mesh, in_specs=in_specs, out_specs=out_specs, check_vma=False
    )
```

```python
import functools

import jax
import jax.numpy as jnp
from jax import lax
from jax.experimental import pallas as pl
from jax.experimental.pallas import tpu as pltpu
from jax.sharding import PartitionSpec as P

HD = 64
PAIR = 2 * HD
BLOCK = 256
WIDE = 512
LANES = 4
F32 = jnp.float32
BF16 = jnp.bfloat16


def remote(src, dst, send_sem, recv_sem, peer):
    return pltpu.make_async_remote_copy(
        src_ref=src,
        dst_ref=dst,
        send_sem=send_sem,
        recv_sem=recv_sem,
        device_id={"xline": peer},
        device_id_type=pl.DeviceIdType.MESH,
    )


def kernel(
    n, rows, cols, width,
    tok, gain_hbm, bias_hbm, w_qkv_hbm, w_out_hbm, out,
    recv, res, gain, bias, w_qkv, w_out, normed, qkv, att,
    in_send, in_recv, out_send, out_recv, w_sem, ready, paired,
):
    me = lax.axis_index("xline")
    length = n * cols
    block = min(BLOCK, length)
    per = block // cols

    loads = [
        pltpu.make_async_copy(far, near, w_sem.at[i])
        for i, (far, near) in enumerate(
            ((w_qkv_hbm, w_qkv), (w_out_hbm, w_out), (gain_hbm, gain), (bias_hbm, bias))
        )
    ]

    def all_of(ref, sem):
        return pltpu.make_async_copy(ref, ref, sem)

    def each_peer(body, unroll=False, near=True, far=True):
        half = n // 2
        side = me // half

        if far:
            @pl.loop(0, half, unroll=unroll)
            def _(k):
                depth = half - 1 - k
                peer = jnp.where(side == 0, half + depth, half - 1 - depth)
                lane = lax.rem(me, 4)
                q = lax.rem(k, 4)
                lane = 2 * lax.rem(lane // 2 + 1 - q // 2, 2) + lax.rem(lane + q, 2)
                body(peer - lax.rem(peer, 4) + lane)

        if near:
            @pl.loop(1, half, unroll=unroll)
            def _(k):
                body(side * half + lax.rem(me + k, half))

    barrier = pltpu.get_barrier_semaphore()
    half = n // 2
    inner = jnp.logical_and(me >= half - LANES, me < half + LANES)
    across = jnp.where(me < half, me + LANES, me - LANES)
    across_sibling = across + 1 - 2 * lax.rem(across, 2)
    sibling = me + 1 - 2 * lax.rem(me, 2)

    def greet(peer, sem=barrier):
        pl.semaphore_signal(
            sem, inc=1, device_id={"xline": peer}, device_id_type=pl.DeviceIdType.MESH
        )

    def send_row(r, peer):
        remote(
            tok.at[peer * rows + r], recv.at[r, me], in_send.at[0], in_recv.at[r], peer
        ).start()

    @pl.when(inner)
    def _():
        greet(across)
        greet(sibling)

    @pl.when(inner)
    def _():
        pl.semaphore_wait(barrier, 2)
        greet(sibling, paired)
        for r in range(rows):
            send_row(r, across)
        pl.semaphore_wait(paired, 1)
        for r in range(rows):
            send_row(r, across_sibling)

    @pl.loop(0, n - 2 * LANES)
    def _(k):
        peer = jnp.where(k < half - LANES, k, k + 2 * LANES)

        @pl.when(peer != me)
        def _():
            greet(peer)

    @pl.loop(0, rows)
    def _(r):
        pltpu.make_async_copy(tok.at[me * rows + r], recv.at[r, me], in_recv.at[r]).start()

    @pl.when(jnp.logical_not(inner))
    def _():
        pl.semaphore_wait(barrier, n - 1)
        side = jnp.where(me < half, 1, -1)
        near = me + side * LANES

        @pl.when(jnp.logical_and(near >= half - LANES, near < half + LANES))
        def _():
            greet(near, ready)

    @pl.when(inner)
    def _():
        pl.semaphore_wait(ready, 1)

    @pl.loop(0, rows)
    def _(r):
        def send(peer):
            done = jnp.logical_and(inner, peer // 2 == across // 2)

            @pl.when(jnp.logical_not(done))
            def _():
                send_row(r, peer)

        each_peer(send, unroll=True, near=False)

    @pl.loop(0, rows)
    def _(r):
        def send(peer):
            done = jnp.logical_and(inner, peer // 2 == across // 2)

            @pl.when(jnp.logical_not(done))
            def _():
                send_row(r, peer)

        each_peer(send, unroll=True, far=False)

    for load in loads:
        load.start()
    for load in loads:
        load.wait()
    low = lax.broadcasted_iota(jnp.int32, (1, PAIR), 1) < HD

    @pl.loop(0, rows)
    def _(r):
        all_of(recv.at[r], in_recv.at[r]).wait()

        @pl.loop(0, length // block)
        def _(b):
            here = pl.ds(pl.multiple_of(b * block, block), block)
            values = recv[r, pl.ds(b * per, per)].astype(F32).reshape(block, width)
            center = jnp.mean(values, axis=-1, keepdims=True)
            moved = values - center
            spread = jnp.mean(moved * moved, axis=-1, keepdims=True)
            normed[...] = (moved * lax.rsqrt(spread + 1e-05) * gain[...] + bias[...]).astype(BF16)

            @pl.loop(0, 3 * width // WIDE)
            def _(c):
                at = pl.ds(pl.multiple_of(c * WIDE, WIDE), WIDE)
                qkv[here, at] = jnp.dot(
                    normed[...], w_qkv[:, at], preferred_element_type=F32
                ).astype(BF16)

        @pl.loop(0, length // block)
        def _(b):
            here = pl.ds(pl.multiple_of(b * block, block), block)

            @pl.loop(0, width // PAIR)
            def _(h):
                q = qkv[here, pl.ds(pl.multiple_of(h * PAIR, PAIR), PAIR)].astype(F32) * 0.125
                keys = qkv[:, pl.ds(pl.multiple_of(width + h * PAIR, PAIR), PAIR)]
                vals = qkv[:, pl.ds(pl.multiple_of(2 * width + h * PAIR, PAIR), PAIR)]
                halves = []
                for mask in (low, jnp.logical_not(low)):
                    one = jnp.where(mask, q, 0.0).astype(BF16)
                    scores = lax.dot_general(
                        one, keys, (((1,), (1,)), ((), ())), preferred_element_type=F32
                    )
                    top = jnp.max(scores, axis=-1, keepdims=True)
                    weights = jnp.exp(scores - top)
                    total = jnp.sum(weights, axis=-1, keepdims=True)
                    mixed = jnp.dot(weights.astype(BF16), vals, preferred_element_type=F32)
                    halves.append(mixed / total)
                att[:, pl.ds(pl.multiple_of(h * PAIR, PAIR), PAIR)] = jnp.where(
                    low, halves[0], halves[1]
                ).astype(BF16)

            @pl.loop(0, width // WIDE)
            def _(c):
                at = pl.ds(pl.multiple_of(c * WIDE, WIDE), WIDE)
                projected = jnp.dot(
                    att[...], w_out[:, at], preferred_element_type=F32
                ).astype(BF16)
                tokens = recv[r, pl.ds(b * per, per), :, at].astype(F32)
                res[r, pl.ds(b * per, per), :, at] = (
                    tokens + projected.astype(F32).reshape(per, cols, WIDE)
                ).astype(BF16)

        pltpu.make_async_copy(res.at[r, me], out.at[me * rows + r], out_recv.at[0]).start()

        def send(peer):
            remote(
                res.at[r, peer], out.at[me * rows + r], out_send.at[0], out_recv.at[0], peer
            ).start()

        each_peer(send)

    sent = tok.at[pl.ds(0, rows * (n - 1))]
    all_of(sent, in_send.at[0]).wait()
    all_of(sent, out_send.at[0]).wait()
    all_of(out, out_recv.at[0]).wait()


def on_device(tokens, norm_gain, norm_bias, w_qkv, w_out):
    inline_rows, cols, width = tokens.shape
    n = lax.axis_size("xline")
    rows = inline_rows // n
    length = n * cols
    anywhere = pl.BlockSpec(memory_space=pl.ANY)
    dma = pltpu.SemaphoreType.DMA
    return pl.pallas_call(
        functools.partial(kernel, n, rows, cols, width),
        out_shape=pltpu.VMEM(tokens.shape, tokens.dtype),
        in_specs=[pl.BlockSpec(memory_space=pltpu.HBM)] * 5,
        out_specs=pl.BlockSpec(memory_space=pltpu.VMEM),
        scratch_shapes=[
            pltpu.VMEM((rows, n, cols, width), BF16),
            pltpu.VMEM((rows, n, cols, width), BF16),
            pltpu.VMEM((1, width), F32),
            pltpu.VMEM((1, width), F32),
            pltpu.VMEM(w_qkv.shape, BF16),
            pltpu.VMEM(w_out.shape, BF16),
            pltpu.VMEM((min(BLOCK, length), width), BF16),
            pltpu.VMEM((length, 3 * width), BF16),
            pltpu.VMEM((min(BLOCK, length), width), BF16),
            dma((1,)),
            dma((rows,)),
            dma((1,)),
            dma((1,)),
            dma((4,)),
            pltpu.SemaphoreType.REGULAR,
            pltpu.SemaphoreType.REGULAR,
        ],
        compiler_params=pltpu.CompilerParams(
            collective_id=0, has_side_effects=True, vmem_limit_bytes=52 * 2**20
        ),
    )(tokens, norm_gain.reshape(1, width), norm_bias.reshape(1, width), w_qkv, w_out)


def solution(mesh):
    in_specs = (P("group", "xline", None), P(), P(), P(), P())
    out_specs = P("group", "xline", None)
    return jax.shard_map(
        on_device, mesh=mesh, in_specs=in_specs, out_specs=out_specs, check_vma=False
    )
```

```python
import functools

import jax
import jax.numpy as jnp
from jax import lax
from jax.experimental import pallas as pl
from jax.experimental.pallas import tpu as pltpu
from jax.sharding import PartitionSpec as P

HD = 64
PAIR = 2 * HD
BLOCK = 256
WIDE = 512
LANES = 4
F32 = jnp.float32
BF16 = jnp.bfloat16


def remote(src, dst, send_sem, recv_sem, peer):
    return pltpu.make_async_remote_copy(
        src_ref=src,
        dst_ref=dst,
        send_sem=send_sem,
        recv_sem=recv_sem,
        device_id={"xline": peer},
        device_id_type=pl.DeviceIdType.MESH,
    )


def kernel(
    n, rows, cols, width,
    tok, gain_hbm, bias_hbm, w_qkv_hbm, w_out_hbm, out,
    recv, res, gain, bias, w_qkv, w_out, normed, qkv, att,
    in_send, in_recv, out_send, out_recv, w_sem, ready, paired,
):
    me = lax.axis_index("xline")
    length = n * cols
    block = min(BLOCK, length)
    per = block // cols

    loads = [
        pltpu.make_async_copy(far, near, w_sem.at[i])
        for i, (far, near) in enumerate(
            ((w_qkv_hbm, w_qkv), (w_out_hbm, w_out), (gain_hbm, gain), (bias_hbm, bias))
        )
    ]

    def all_of(ref, sem):
        return pltpu.make_async_copy(ref, ref, sem)

    def each_peer(body, unroll=False, near=True, far=True):
        half = n // 2
        side = me // half

        if far:
            @pl.loop(0, half, unroll=unroll)
            def _(k):
                depth = half - 1 - k
                peer = jnp.where(side == 0, half + depth, half - 1 - depth)
                lane = lax.rem(me, 4)
                q = lax.rem(k, 4)
                lane = 2 * lax.rem(lane // 2 + 1 - q // 2, 2) + lax.rem(lane + q, 2)
                body(peer - lax.rem(peer, 4) + lane)

        if near:
            @pl.loop(1, half, unroll=unroll)
            def _(k):
                body(side * half + lax.rem(me + k, half))

    barrier = pltpu.get_barrier_semaphore()
    half = n // 2
    inner = jnp.logical_and(me >= half - LANES, me < half + LANES)
    across = jnp.where(me < half, me + LANES, me - LANES)
    across_sibling = across + 1 - 2 * lax.rem(across, 2)
    sibling = me + 1 - 2 * lax.rem(me, 2)

    def greet(peer, sem=barrier):
        pl.semaphore_signal(
            sem, inc=1, device_id={"xline": peer}, device_id_type=pl.DeviceIdType.MESH
        )

    def send_row(r, peer):
        remote(
            tok.at[peer * rows + r], recv.at[r, me], in_send.at[0], in_recv.at[r], peer
        ).start()

    @pl.when(inner)
    def _():
        greet(across)
        greet(sibling)

    @pl.loop(0, n - 2 * LANES)
    def _(k):
        peer = jnp.where(k < half - LANES, k, k + 2 * LANES)

        @pl.when(peer != me)
        def _():
            greet(peer)

    @pl.when(inner)
    def _():
        pl.semaphore_wait(barrier, 2)
        greet(sibling, paired)
        for r in range(rows):
            send_row(r, across)
        pl.semaphore_wait(paired, 1)
        for r in range(rows):
            send_row(r, across_sibling)

    @pl.when(jnp.logical_not(inner))
    def _():
        pl.semaphore_wait(barrier, n - 1)
        side = jnp.where(me < half, 1, -1)
        near = me + side * LANES

        @pl.when(jnp.logical_and(near >= half - LANES, near < half + LANES))
        def _():
            greet(near, ready)

    @pl.when(inner)
    def _():
        pl.semaphore_wait(ready, 1)

    @pl.loop(0, rows)
    def _(r):
        def send(peer):
            done = jnp.logical_and(inner, peer // 2 == across // 2)

            @pl.when(jnp.logical_not(done))
            def _():
                send_row(r, peer)

        each_peer(send, unroll=True, near=False)

    @pl.loop(0, rows)
    def _(r):
        def send(peer):
            done = jnp.logical_and(inner, peer // 2 == across // 2)

            @pl.when(jnp.logical_not(done))
            def _():
                send_row(r, peer)

        each_peer(send, unroll=True, far=False)

    @pl.loop(0, rows)
    def _(r):
        pltpu.make_async_copy(tok.at[me * rows + r], recv.at[r, me], in_recv.at[r]).start()

    for load in loads:
        load.start()
    for load in loads:
        load.wait()
    low = lax.broadcasted_iota(jnp.int32, (1, PAIR), 1) < HD

    @pl.loop(0, rows)
    def _(r):
        all_of(recv.at[r], in_recv.at[r]).wait()

        @pl.loop(0, length // block)
        def _(b):
            here = pl.ds(pl.multiple_of(b * block, block), block)
            values = recv[r, pl.ds(b * per, per)].astype(F32).reshape(block, width)
            center = jnp.mean(values, axis=-1, keepdims=True)
            moved = values - center
            spread = jnp.mean(moved * moved, axis=-1, keepdims=True)
            normed[...] = (moved * lax.rsqrt(spread + 1e-05) * gain[...] + bias[...]).astype(BF16)

            @pl.loop(0, 3 * width // WIDE)
            def _(c):
                at = pl.ds(pl.multiple_of(c * WIDE, WIDE), WIDE)
                qkv[here, at] = jnp.dot(
                    normed[...], w_qkv[:, at], preferred_element_type=F32
                ).astype(BF16)

        @pl.loop(0, length // block)
        def _(b):
            here = pl.ds(pl.multiple_of(b * block, block), block)

            @pl.loop(0, width // PAIR)
            def _(h):
                q = qkv[here, pl.ds(pl.multiple_of(h * PAIR, PAIR), PAIR)].astype(F32) * 0.125
                keys = qkv[:, pl.ds(pl.multiple_of(width + h * PAIR, PAIR), PAIR)]
                vals = qkv[:, pl.ds(pl.multiple_of(2 * width + h * PAIR, PAIR), PAIR)]
                halves = []
                for mask in (low, jnp.logical_not(low)):
                    one = jnp.where(mask, q, 0.0).astype(BF16)
                    scores = lax.dot_general(
                        one, keys, (((1,), (1,)), ((), ())), preferred_element_type=F32
                    )
                    top = jnp.max(scores, axis=-1, keepdims=True)
                    weights = jnp.exp(scores - top)
                    total = jnp.sum(weights, axis=-1, keepdims=True)
                    mixed = jnp.dot(weights.astype(BF16), vals, preferred_element_type=F32)
                    halves.append(mixed / total)
                att[:, pl.ds(pl.multiple_of(h * PAIR, PAIR), PAIR)] = jnp.where(
                    low, halves[0], halves[1]
                ).astype(BF16)

            @pl.loop(0, width // WIDE)
            def _(c):
                at = pl.ds(pl.multiple_of(c * WIDE, WIDE), WIDE)
                projected = jnp.dot(
                    att[...], w_out[:, at], preferred_element_type=F32
                ).astype(BF16)
                tokens = recv[r, pl.ds(b * per, per), :, at].astype(F32)
                res[r, pl.ds(b * per, per), :, at] = (
                    tokens + projected.astype(F32).reshape(per, cols, WIDE)
                ).astype(BF16)

        pltpu.make_async_copy(res.at[r, me], out.at[me * rows + r], out_recv.at[0]).start()

        def send(peer):
            remote(
                res.at[r, peer], out.at[me * rows + r], out_send.at[0], out_recv.at[0], peer
            ).start()

        each_peer(send)

    sent = tok.at[pl.ds(0, rows * (n - 1))]
    all_of(sent, in_send.at[0]).wait()
    all_of(sent, out_send.at[0]).wait()
    all_of(out, out_recv.at[0]).wait()


def on_device(tokens, norm_gain, norm_bias, w_qkv, w_out):
    inline_rows, cols, width = tokens.shape
    n = lax.axis_size("xline")
    rows = inline_rows // n
    length = n * cols
    anywhere = pl.BlockSpec(memory_space=pl.ANY)
    dma = pltpu.SemaphoreType.DMA
    return pl.pallas_call(
        functools.partial(kernel, n, rows, cols, width),
        out_shape=pltpu.VMEM(tokens.shape, tokens.dtype),
        in_specs=[pl.BlockSpec(memory_space=pltpu.HBM)] * 5,
        out_specs=pl.BlockSpec(memory_space=pltpu.VMEM),
        scratch_shapes=[
            pltpu.VMEM((rows, n, cols, width), BF16),
            pltpu.VMEM((rows, n, cols, width), BF16),
            pltpu.VMEM((1, width), F32),
            pltpu.VMEM((1, width), F32),
            pltpu.VMEM(w_qkv.shape, BF16),
            pltpu.VMEM(w_out.shape, BF16),
            pltpu.VMEM((min(BLOCK, length), width), BF16),
            pltpu.VMEM((length, 3 * width), BF16),
            pltpu.VMEM((min(BLOCK, length), width), BF16),
            dma((1,)),
            dma((rows,)),
            dma((1,)),
            dma((1,)),
            dma((4,)),
            pltpu.SemaphoreType.REGULAR,
            pltpu.SemaphoreType.REGULAR,
        ],
        compiler_params=pltpu.CompilerParams(
            collective_id=0, has_side_effects=True, vmem_limit_bytes=52 * 2**20
        ),
    )(tokens, norm_gain.reshape(1, width), norm_bias.reshape(1, width), w_qkv, w_out)


def solution(mesh):
    in_specs = (P("group", "xline", None), P(), P(), P(), P())
    out_specs = P("group", "xline", None)
    return jax.shard_map(
        on_device, mesh=mesh, in_specs=in_specs, out_specs=out_specs, check_vma=False
    )
```
